256 devices in a mesh: elec: 4 (over z_hi, core), row: 16 (over z_lo, y), col: 4 (over x).
Axes of the slice: x: 4, y: 4, z: 8 (z_hi: 2, z_lo: 4; z = z_hi * 4 + z_lo), core: 2. Of those that a mesh axis runs over, the one named last changes fastest.
Arguments:
- fields: bfloat16 [256, 2, 512, 256], P(('elec', 'row', 'col')), may hold values from -6 to 6
- mirror_phase: float32 [512, 256], replicated, may hold values from -3.140625 to 3.140625
- tile_list: int32 [16, 4, 9, 2], P('row', 'col'), may hold values from -1 to 31, as said below
Outputs:
- csd_tiles: float32 [16, 4, 9, 2, 768, 768], P('row', 'col', None, None, 'elec')
The draws below stay inside these ranges and needn't reach their ends.
Inputs may be any that keep to these rules, and one draw needn't show every extreme that they name: `tile_list`: each slot of row index r and col index c holds a tile (i, j) of the lower triangle, j <= i, with i equal to r or 31 - r and j congruent to c modulo the number of col indices; every such tile appears in exactly one slot of its r and c, in drawn order; the other slots hold -1 in both entries.
All inputs are finite; a program needn't handle non-finite values.
Results may differ from the reference program's by a relative error of at most 0.012.
Values may be sent and summed in bfloat16 or wider, within the bound.
No kernel may reach another device: no remote copies, remote signals or barrier semaphores. Data moves between devices by JAX's collectives and lax.ppermute only.
A program may use at most 192 MiB of HBM per device.

```python
import math
import jax
import jax.numpy as jnp
from jax import lax

NX = 512
NY = 256
TILE = 768
NE = 256
NT = 32
WIN = 24576
SLAB_ROWS = 96
SLOTS = 9
N_ROW = 16
N_COL = 4


def draw_tile_list(key, part):
    spread = NT // N_COL

    def one_device(device_key, row_index, col_index):
        candidate = jnp.arange(2 * spread, dtype=jnp.int32)
        high_side = candidate // spread
        tile_row = jnp.where(high_side == 0, row_index, NT - 1 - row_index)
        tile_col = col_index + N_COL * (candidate % spread)
        listed = (tile_col <= tile_row).astype(jnp.int32)
        split_keys = jax.random.split(device_key, 2)
        order_score = (1 - listed) * (2 * spread) + jax.random.permutation(split_keys[0], 2 * spread).astype(jnp.int32)
        ranked = jnp.argsort(order_score, stable=True)[:SLOTS]
        rows_pick = jnp.where(listed[ranked] == 1, tile_row[ranked], -1)
        cols_pick = jnp.where(listed[ranked] == 1, tile_col[ranked], -1)
        shuffle = jax.random.permutation(split_keys[1], SLOTS)
        return jnp.stack([rows_pick[shuffle], cols_pick[shuffle]], axis=1)
    grid_rows = jnp.repeat(jnp.arange(N_ROW, dtype=jnp.int32), N_COL)
    grid_cols = jnp.tile(jnp.arange(N_COL, dtype=jnp.int32), N_ROW)
    device_keys = jax.random.split(jax.random.fold_in(key, 17), N_ROW * N_COL)
    listing = jax.vmap(one_device)(device_keys, grid_rows, grid_cols)
    return listing.reshape(N_ROW, N_COL, SLOTS, 2).astype(jnp.int32)


def shard_levels(rng, shape, pieces, least, high):
    def one(dim, shards_of):
        draws = jax.random.uniform(jax.random.fold_in(jax.random.fold_in(rng, 6), dim), (shards_of,), jnp.float32, least / len(pieces), high / len(pieces))
        return jnp.repeat(jnp.exp(draws), shape[dim] // shards_of).reshape((-1,) + (1,) * (len(shape) - dim - 1))

    loudness = one(*pieces[0])
    for cut in pieces[1:]:
        loudness = loudness * one(*cut)
    return loudness


def centred(rng, shape, deviation, most, shards=(), kind=jnp.bfloat16):
    array = deviation * jax.random.normal(rng, shape, jnp.float32)
    if shards:
        array = array * shard_levels(rng, shape, shards, -0.22, 0.18)
    return jnp.clip(array, -most, most).astype(kind)


def setup_inputs(seed: int = 0) -> dict:
    arg_keys = jax.random.split(jax.random.key(seed), 4)
    fields = centred(arg_keys[0], (NE, 2, NX, NY), 1.0, 6.0, ((0, 256),))
    mirror_phase = jnp.clip(jax.random.uniform(arg_keys[1], (NX, NY), jnp.float32, -3.140625, 3.140625), -3.140625, 3.140625)
    tile_list = draw_tile_list(jax.random.fold_in(arg_keys[3], 71), 0)
    return {"fields": fields, "mirror_phase": mirror_phase, "tile_list": tile_list}


def dft_parts(length, sign_value):
    positions = jnp.arange(length, dtype=jnp.int32)
    product = positions[:, None] * positions[None, :] % length
    angles = 2.0 * math.pi / length * product.astype(jnp.float32)
    factor = 1.0 / math.sqrt(length)
    return (jnp.cos(angles) * factor, sign_value * jnp.sin(angles) * factor)

def left_table(length, sign_value, row_limit):
    real_part, imag_part = dft_parts(length, sign_value)
    real_part = real_part[:row_limit]
    imag_part = imag_part[:row_limit]
    return jnp.stack([jnp.stack([real_part, -imag_part]), jnp.stack([imag_part, real_part])]).astype(jnp.bfloat16)

def right_table(length, sign_value):
    real_part, imag_part = dft_parts(length, sign_value)
    return jnp.stack([jnp.stack([real_part, imag_part]), jnp.stack([-imag_part, real_part])]).astype(jnp.bfloat16)

def contract(formula, left_side, right_side):
    return jnp.einsum(formula, left_side.astype(jnp.float32), right_side.astype(jnp.float32), precision=lax.Precision.HIGHEST)

def reference(fields, mirror_phase, tile_list):
    cos_phase = jnp.cos(mirror_phase)
    sin_phase = jnp.sin(mirror_phase)
    forward_left = left_table(NX, -1.0, NX)
    forward_right = right_table(NY, -1.0)
    inverse_left = left_table(NX, 1.0, SLAB_ROWS)
    inverse_right = right_table(NY, 1.0)

    def propagate_one(single):
        first_pass = contract('dcwx,cxy->dwy', forward_left, single).astype(jnp.bfloat16)
        turned = contract('cxy,cdyz->dxz', first_pass, forward_right)
        spectrum = jnp.stack([turned[0] * cos_phase - turned[1] * sin_phase, turned[0] * sin_phase + turned[1] * cos_phase]).astype(jnp.bfloat16)
        back_rows = contract('dcwx,cxy->dwy', inverse_left, spectrum).astype(jnp.bfloat16)
        slab_part = contract('cxy,cdyz->dxz', back_rows, inverse_right).astype(jnp.bfloat16)
        return slab_part.reshape(2, WIN)
    slab_field = lax.map(propagate_one, fields)
    entries = tile_list.reshape(-1, 2)
    scale = 1.0 / math.sqrt(NE)

    def one_tile(entry):
        tile_row = entry[0]
        tile_col = entry[1]
        row_start = (jnp.maximum(tile_row, 0) * TILE).astype(jnp.int32)
        col_start = (jnp.maximum(tile_col, 0) * TILE).astype(jnp.int32)
        rows_part = lax.dynamic_slice_in_dim(slab_field, row_start, TILE, 2).astype(jnp.float32)
        cols_part = lax.dynamic_slice_in_dim(slab_field, col_start, TILE, 2).astype(jnp.float32)
        real_sum = contract('ep,eq->qp', rows_part[:, 0], cols_part[:, 0]) + contract('ep,eq->qp', rows_part[:, 1], cols_part[:, 1])
        imag_sum = contract('ep,eq->qp', rows_part[:, 1], cols_part[:, 0]) - contract('ep,eq->qp', rows_part[:, 0], cols_part[:, 1])
        result = jnp.stack([real_sum, imag_sum]) * scale
        return jnp.where(tile_row >= 0, result, jnp.zeros_like(result))
    tiles = lax.map(one_tile, entries)
    return tiles.reshape(N_ROW, N_COL, SLOTS, 2, TILE, TILE)
```

```python
import math

import jax
import jax.numpy as jnp
import numpy as np
from jax import lax
from jax.experimental import pallas as pl
from jax.experimental.pallas import tpu as pltpu
from jax.sharding import Mesh, PartitionSpec as P

NX = 512
NY = 256
TILE = 768
QUARTER = 192
SLOTS = 9
ROWS = 24
LANES = 128
AXES = ("zh", "k", "zl", "y", "x")


def dft_parts(length):
    positions = np.arange(length, dtype=np.int32)
    product = positions[:, None] * positions[None, :] % length
    angles = (np.float32(2.0 * math.pi / length) * product.astype(np.float32)).astype(np.float32)
    factor = np.float32(1.0 / math.sqrt(length))
    return np.cos(angles) * factor, np.sin(angles) * factor


def tables():
    bf16 = jnp.bfloat16
    cos_x, sin_x = dft_parts(NX)
    cos_y, sin_y = dft_parts(NY)
    inverse = np.zeros((192, 2 * NX), np.float32)
    turn = np.zeros((192, 192), np.float32)
    order = np.zeros((192, 192), np.float32)

    def place(tile, part, w):
        r, u = (tile, 0) if tile < 16 else (31 - tile, 1)
        return ((r * 2 + u) * 2 + part) * 3 + w

    for tile in range(32):
        for w in range(3):
            line = tile * 3 + w
            re, im = place(tile, 0, w), place(tile, 1, w)
            inverse[re] = np.concatenate([cos_x[line], -sin_x[line]])
            inverse[im] = np.concatenate([sin_x[line], cos_x[line]])
            turn[re, im] = -1.0
            turn[im, re] = 1.0
            for part in range(2):
                m, x = divmod(tile, 4)
                target = ((((w * 4 + x) * 2 + m % 2) * 4 + m // 2) * 2) + part
                order[target, place(tile, part, w)] = 1.0
    return [jnp.asarray(a, bf16) for a in (cos_x, sin_x, cos_y, sin_y, inverse, turn, order)]


def dot(a, b):
    return jnp.dot(a, b, preferred_element_type=jnp.float32)


def cos_sin(theta):
    h = theta * 0.5
    s = h * h
    sin_h = h * (1.0 + s * (-1.0 / 6 + s * (1.0 / 120 + s * (-1.0 / 5040 + s * (1.0 / 362880 + s * (-1.0 / 39916800))))))
    cos_h = 1.0 + s * (-0.5 + s * (1.0 / 24 + s * (-1.0 / 720 + s * (1.0 / 40320 + s * (-1.0 / 3628800 + s * (1.0 / 479001600))))))
    return 1.0 - 2.0 * sin_h * sin_h, 2.0 * sin_h * cos_h


def front_kernel(fields, phase, cos_x, sin_x, cos_y, sin_y, inverse, turn, order, row_out, col_out):
    bf16 = jnp.bfloat16
    xr = fields[0, 0]
    xi = fields[0, 1]
    cx = cos_x[...]
    sx = sin_x[...]
    first_r = (dot(cx, xr) + dot(sx, xi)).astype(bf16)
    first_i = (dot(cx, xi) - dot(sx, xr)).astype(bf16)
    cy = cos_y[...]
    sy = sin_y[...]
    turned_r = dot(first_r, cy) + dot(first_i, sy)
    turned_i = dot(first_i, cy) - dot(first_r, sy)
    cos_p, sin_p = cos_sin(phase[...])
    spec_r = (turned_r * cos_p - turned_i * sin_p).astype(bf16)
    spec_i = (turned_r * sin_p + turned_i * cos_p).astype(bf16)
    inv = inverse[...]
    back = (dot(inv[:, :NX], spec_r) + dot(inv[:, NX:], spec_i)).astype(bf16)
    back_turned = dot(turn[...], back).astype(bf16)
    slab = dot(back, cy) + dot(back_turned, sy)
    slab_b = slab.astype(bf16)
    slab_r = slab_b.astype(jnp.float32)
    slab_c = dot(order[...], slab_b)
    for r in range(16):
        for h in range(2):
            piece = slab_r[r * 12:(r + 1) * 12, h * LANES:(h + 1) * LANES].astype(bf16)
            for zh in range(2):
                row_out[zh * 16 + r, h * 12:(h + 1) * 12, :] = piece
    low = lax.broadcasted_iota(jnp.int32, (8, LANES), 1) < 64
    wide = ((0, 0), (1, 0), (1, 1), (2, 1))
    slim = ((0, 1), (0, 1), (2, 0), (2, 0))
    for x in range(4):
        for zh in range(2):
            for k in range(2):
                q = zh * 2 + k
                w, h = wide[q]
                base = w * 64 + x * 16
                a = slab_c[base:base + 16, h * LANES:(h + 1) * LANES].astype(bf16)
                w, h = slim[q]
                base = w * 64 + x * 16
                even = slab_c[base:base + 8, h * LANES:(h + 1) * LANES]
                odd = slab_c[base + 8:base + 16, h * LANES:(h + 1) * LANES]
                if k == 0:
                    b = jnp.where(low, even, pltpu.roll(odd, 64, 1))
                else:
                    b = jnp.where(low, pltpu.roll(even, 64, 1), odd)
                b = b.astype(bf16)
                for zl in range(4):
                    dest = ((k * 4 + x) * 2 + zh) * 4 + zl
                    col_out[dest, 0:16, :] = a
                    col_out[dest, 16:24, :] = b


def front(fields, phase):
    return pl.pallas_call(
        front_kernel,
        out_shape=[
            jax.ShapeDtypeStruct((32, ROWS, LANES), jnp.bfloat16),
            jax.ShapeDtypeStruct((64, ROWS, LANES), jnp.bfloat16),
        ],
        name="front",
    )(fields, phase, *tables())


def back_kernel(tiles, where, rows, cols, out, row_f, col_f, row_s, col_s):
    bf16 = jnp.bfloat16

    @pl.when(pl.program_id(0) == 0)
    def _():
        core = where[0]
        x_at = where[1]
        y_at = where[2]

        def slot(a, b):
            d = a ^ b
            return jnp.where(d == 2, 3, jnp.where(d == 3, 2, d))

        def spread(g, carry):
            row_f[pl.ds(g * 8 * ROWS, 8 * ROWS), :] = rows[pl.ds(g * 8, 8)].reshape(8 * ROWS, LANES).astype(jnp.float32)
            col_f[pl.ds(g * 8 * ROWS, 8 * ROWS), :] = cols[pl.ds(g * 8, 8)].reshape(8 * ROWS, LANES).astype(jnp.float32)
            return carry

        lax.fori_loop(0, 32, spread, 0)

        def gather(g, carry):
            y = g // 4
            k = (g // 2) % 2
            xp = g % 2
            e0 = pl.multiple_of(g * 16, 16)
            cbase = (slot(y, y_at) * 64 + k * 32 + xp * 16) * ROWS
            r0 = (((k ^ core) * 4 + slot(xp * 2, x_at)) * 32 + y) * ROWS
            r1 = (((k ^ core) * 4 + slot(xp * 2 + 1, x_at)) * 32 + y) * ROWS
            for u in range(2):
                for c in range(2):
                    for w in range(3):
                        for h in range(2):
                            rho = h * 12 + (u * 2 + c) * 3 + w
                            v = jnp.concatenate(
                                [
                                    row_f[pl.ds(r0 + rho, 8, stride=4 * ROWS), :],
                                    row_f[pl.ds(r1 + rho, 8, stride=4 * ROWS), :],
                                ],
                                axis=0,
                            )
                            lane = (w * 2 + h) * LANES
                            row_s[u, pl.ds(c * 256 + e0, 16), lane:lane + LANES] = v.astype(bf16)
            for rho in range(ROWS):
                v = jnp.concatenate(
                    [
                        col_f[pl.ds(cbase + rho, 8, stride=ROWS), :],
                        col_f[pl.ds(cbase + 8 * ROWS + rho, 8, stride=ROWS), :],
                    ],
                    axis=0,
                )
                col_s[rho, pl.ds(e0, 16), :] = v.astype(bf16)
            return carry

        lax.fori_loop(0, 16, gather, 0)

    slot_id = pl.program_id(0)
    tile_row = tiles[slot_id, 0]
    tile_col = tiles[slot_id, 1]
    return tile_row, tile_col


def back_body(tiles, where, rows, cols, out, row_f, col_f, row_s, col_s, left):
    bf16 = jnp.bfloat16
    tile_row, tile_col = back_kernel(tiles, where, rows, cols, out, row_f, col_f, row_s, col_s)

    @pl.when(pl.program_id(0) == 0)
    def _():
        core = where[0]
        wide_at = core * 64
        slim_at = (1 - core) * 128

        def put(m, at, size, re, im):
            neg = -im
            left[m, pl.ds(at, size), 0:256] = re
            left[m, pl.ds(at, size), 256:512] = im
            left[m, pl.ds(QUARTER + at, size), 0:256] = neg
            left[m, pl.ds(QUARTER + at, size), 256:512] = re

        for mp in range(4):
            for par in range(2):
                rho = (par * 4 + mp) * 2
                re = jnp.transpose(col_s[rho])
                im = jnp.transpose(col_s[rho + 1])
                put(2 * mp + par, pl.multiple_of(wide_at, 64), 128, re, im)
            rho = 16 + mp * 2
            re = jnp.transpose(col_s[rho])
            im = jnp.transpose(col_s[rho + 1])
            for par in range(2):
                part = slice(par * 64, par * 64 + 64)
                put(2 * mp + par, pl.multiple_of(slim_at, 64), 64, re[part], im[part])

    @pl.when(tile_row >= 0)
    def _():
        u = (tile_row >= 16).astype(jnp.int32)
        m = tile_col // 4
        res = dot(left[m], row_s[u]) * 0.0625
        out[0, 0, 0, 0] = res[:QUARTER]
        out[0, 0, 0, 1] = res[QUARTER:]

    @pl.when(tile_row < 0)
    def _():
        out[...] = jnp.zeros_like(out)


def back(tiles, where, rows, cols):
    return pl.pallas_call(
        back_body,
        grid_spec=pltpu.PrefetchScalarGridSpec(
            num_scalar_prefetch=2,
            grid=(SLOTS,),
            in_specs=[
                pl.BlockSpec((256, ROWS, LANES), lambda s, *_: (0, 0, 0), pipeline_mode=pl.Buffered(1)),
                pl.BlockSpec((256, ROWS, LANES), lambda s, *_: (0, 0, 0), pipeline_mode=pl.Buffered(1)),
            ],
            out_specs=pl.BlockSpec((1, 1, 1, 2, QUARTER, TILE), lambda s, *_: (0, 0, s, 0, 0, 0)),
            scratch_shapes=[
                pltpu.VMEM((256 * ROWS, LANES), jnp.float32),
                pltpu.VMEM((256 * ROWS, LANES), jnp.float32),
                pltpu.VMEM((2, 512, TILE), jnp.bfloat16),
                pltpu.VMEM((ROWS, 256, LANES), jnp.bfloat16),
                pltpu.VMEM((8, 2 * QUARTER, 512), jnp.bfloat16),
            ],
        ),
        out_shape=jax.ShapeDtypeStruct((1, 1, SLOTS, 2, QUARTER, TILE), jnp.float32),
        name="back",
    )(tiles, where, rows, cols)


def swap(value, axis, change):
    return lax.ppermute(value, axis, [(i, change(i)) for i in range(lax.axis_size(axis))])


def spread_over(value, axis):
    near = swap(value, axis, lambda i: i ^ 1)
    pair = jnp.concatenate([value, near], axis=0)
    far = swap(pair, axis, lambda i: 3 - i)
    return jnp.concatenate([pair, far], axis=0)


def body(fields, mirror_phase, tile_list):
    rows, cols = front(fields, mirror_phase)
    cols = lax.all_to_all(cols, ("k", "x", "zh", "zl"), 0, 0, tiled=True)
    rows = lax.all_to_all(rows, ("zh", "zl", "y"), 0, 0, tiled=True)
    cols = spread_over(cols, "y")
    rows = spread_over(rows, "x")
    other = swap(rows, "k", lambda i: 1 - i)
    rows = jnp.concatenate([rows, other], axis=0)
    where = jnp.stack([lax.axis_index("k"), lax.axis_index("x"), lax.axis_index("y")]).astype(jnp.int32)
    return back(tile_list[0, 0], where, rows, cols)


def solution(mesh):
    fine = Mesh(mesh.devices.reshape(2, 2, 4, 4, 4), AXES)
    in_specs = (P(AXES, None, None, None), P(), P(("zl", "y"), "x", None, None))
    out_specs = P(("zl", "y"), "x", None, None, ("zh", "k"), None)
    return jax.shard_map(body, mesh=fine, in_specs=in_specs, out_specs=out_specs, check_vma=False)
```

```python
import math

import jax
import jax.numpy as jnp
import numpy as np
from jax import lax
from jax.experimental import pallas as pl
from jax.experimental.pallas import tpu as pltpu
from jax.sharding import Mesh, PartitionSpec as P


NX = 512
NY = 256
TILE = 768
QUARTER = 192
SLOTS = 9
ROWS = 24
PEER_ROWS = 288
LANES = 128
AXES = ("zh", "k", "zl", "y", "x")


def dft_parts(length):
    positions = np.arange(length, dtype=np.int32)
    product = positions[:, None] * positions[None, :] % length
    angles = (np.float32(2.0 * math.pi / length) * product.astype(np.float32)).astype(np.float32)
    factor = np.float32(1.0 / math.sqrt(length))
    return np.cos(angles) * factor, np.sin(angles) * factor


def tables():
    bf16 = jnp.bfloat16
    cos_x, sin_x = dft_parts(NX)
    cos_y, sin_y = dft_parts(NY)
    inverse = np.zeros((192, 2 * NX), np.float32)
    turn = np.zeros((192, 192), np.float32)
    order = np.zeros((192, 192), np.float32)

    def place(tile, part, w):
        r, u = (tile, 0) if tile < 16 else (31 - tile, 1)
        return (((r % 4 * 4 + r // 4) * 2 + u) * 2 + part) * 3 + w

    for tile in range(32):
        for w in range(3):
            line = tile * 3 + w
            re, im = place(tile, 0, w), place(tile, 1, w)
            inverse[re] = np.concatenate([cos_x[line], -sin_x[line]])
            inverse[im] = np.concatenate([sin_x[line], cos_x[line]])
            turn[re, im] = -1.0
            turn[im, re] = 1.0
            for part in range(2):
                m, x = divmod(tile, 4)
                target = ((((w * 4 + x) * 2 + m % 2) * 4 + m // 2) * 2) + part
                order[target, place(tile, part, w)] = 1.0
    return [jnp.asarray(a, bf16) for a in (cos_x, sin_x, cos_y, sin_y, inverse, turn, order)]


def dot(a, b):
    return jnp.dot(a, b, preferred_element_type=jnp.float32)


def cos_sin(theta):
    h = theta * 0.5
    s = h * h
    sin_h = h * (1.0 + s * (-1.0 / 6 + s * (1.0 / 120 + s * (-1.0 / 5040 + s * (1.0 / 362880 + s * (-1.0 / 39916800))))))
    cos_h = 1.0 + s * (-0.5 + s * (1.0 / 24 + s * (-1.0 / 720 + s * (1.0 / 40320 + s * (-1.0 / 3628800 + s * (1.0 / 479001600))))))
    return 1.0 - 2.0 * sin_h * sin_h, 2.0 * sin_h * cos_h


def front_kernel(fields, phase, cos_x, sin_x, cos_y, sin_y, inverse, turn, order, *rest):
    bf16 = jnp.bfloat16
    row_out = rest[:4]
    col_out = rest[4:8]
    slab_f, slab_c = rest[8:]
    xr = fields[0, 0]
    xi = fields[0, 1]
    cx = cos_x[...]
    sx = sin_x[...]
    first_r = (dot(cx, xr) + dot(sx, xi)).astype(bf16)
    first_i = (dot(cx, xi) - dot(sx, xr)).astype(bf16)
    cy = cos_y[...]
    sy = sin_y[...]
    turned_r = dot(first_r, cy) + dot(first_i, sy)
    turned_i = dot(first_i, cy) - dot(first_r, sy)
    cos_p, sin_p = cos_sin(phase[...])
    spec_r = (turned_r * cos_p - turned_i * sin_p).astype(bf16)
    spec_i = (turned_r * sin_p + turned_i * cos_p).astype(bf16)
    inv = inverse[...]
    back = (dot(inv[:, :NX], spec_r) + dot(inv[:, NX:], spec_i)).astype(bf16)
    back_turned = dot(turn[...], back).astype(bf16)
    slab = (dot(back, cy) + dot(back_turned, sy)).astype(bf16)
    slab_f[...] = slab.astype(jnp.float32)
    slab_c[...] = dot(order[...], slab)
    x_at = lax.axis_index("x")
    y_at = lax.axis_index("y")
    low = lax.broadcasted_iota(jnp.int32, (8, LANES), 1) < 64
    wide = ((0, 0), (1, 0), (1, 1), (2, 1))
    slim = ((0, 1), (0, 1), (2, 0), (2, 0))
    for o in range(4):
        block = slab_f[pl.ds(pl.multiple_of((y_at ^ o) * 48, 8), 48), :]
        for zl in range(4):
            for u in range(2):
                for h in range(2):
                    at = (zl * 2 + u) * 6
                    to = u * 12 + h * 6
                    row_out[o][zl, to:to + 6, :] = block[at:at + 6, h * LANES:(h + 1) * LANES].astype(bf16)
        xb = (x_at ^ o) * 16
        for q in range(4):
            w, h = wide[q]
            a = slab_c[pl.ds(pl.multiple_of(xb + w * 64, 8), 16), h * LANES:(h + 1) * LANES]
            w, h = slim[q]
            e = slab_c[pl.ds(pl.multiple_of(xb + w * 64, 8), 16), h * LANES:(h + 1) * LANES]
            even, odd = e[:8], e[8:]
            if q % 2 == 0:
                b = jnp.where(low, even, pltpu.roll(odd, 64, 1))
            else:
                b = jnp.where(low, pltpu.roll(even, 64, 1), odd)
            col_out[o][q, 0:16, :] = a.astype(bf16)
            col_out[o][q, 16:24, :] = b.astype(bf16)


def vmem(shape, dtype=jnp.bfloat16):
    return pltpu.VMEM(shape, dtype)


def local_call(kernel, outs, args, scratch=()):
    spec = pl.BlockSpec(memory_space=pltpu.VMEM)
    here = [pltpu.with_memory_space_constraint(a, pltpu.VMEM) for a in args]
    return pl.pallas_call(
        kernel,
        out_shape=[vmem(shape) for shape in outs],
        in_specs=[spec] * len(here),
        out_specs=[spec] * len(outs),
        scratch_shapes=list(scratch),
        compiler_params=pltpu.CompilerParams(vmem_limit_bytes=12 << 20),
    )(*here)


def front(fields, phase):
    return pl.pallas_call(
        front_kernel,
        out_shape=[vmem((4, ROWS, LANES))] * 8,
        out_specs=[pl.BlockSpec(memory_space=pltpu.VMEM)] * 8,
        scratch_shapes=[pltpu.VMEM((192, NY), jnp.float32), pltpu.VMEM((192, NY), jnp.float32)],
        name="front",
    )(fields, phase, *tables())


def pack_kernel(*refs):
    rows = refs[:4]
    cols = refs[4:8]
    outs = refs[8:]
    z_at = lax.axis_index("zh") * 4 + lax.axis_index("zl")
    for d, out in enumerate(outs):
        z = (z_at + d) % 8
        zh = z // 4
        zl = z % 4
        for o in range(4):
            for k in range(2):
                to = o * 48 + k * 24
                out[to:to + 24, :] = cols[o][zh * 2 + k]
            to = 192 + o * 24
            out[to:to + 24, :] = rows[o][zl]


def pack(rows, cols):
    return local_call(pack_kernel, [(PEER_ROWS, LANES)] * 8, [*rows, *cols])


def split_kernel(*refs):
    peers = refs[:8]
    mine, theirs, flat = refs[8:]
    bf16 = jnp.bfloat16
    core = lax.axis_index("k")
    for z in range(8):
        flat[z * PEER_ROWS:(z + 1) * PEER_ROWS, :] = peers[z][...].astype(jnp.float32)

    def pair(at, step):
        return jnp.concatenate(
            [flat[pl.ds(at, 8, stride=PEER_ROWS), :], flat[pl.ds(at + step, 8, stride=PEER_ROWS), :]], axis=0
        ).astype(bf16)

    for out, k in ((mine, core), (theirs, 1 - core)):
        for c in range(2):
            for o in range(0, 4, 2):
                to = (c * 4 + o) * 8
                for j in range(12):
                    out[j, to:to + 16, :] = pair(o * 48 + k * 24 + j * 2 + c, 48)
                for w in range(3):
                    for h in range(2):
                        out[12 + w * 2 + h, to:to + 16, :] = pair(192 + o * 24 + k * 12 + h * 6 + c * 3 + w, 24)


def split(peers):
    return local_call(
        split_kernel,
        [(18, 64, LANES)] * 2,
        peers,
        scratch=[pltpu.VMEM((8 * PEER_ROWS, LANES), jnp.float32)],
    )


def merge_kernel(mine, theirs, row_out, col_out):
    bf16 = jnp.bfloat16
    is_first = lax.axis_index("k") == 0
    for j in range(18):
        a = mine[j].astype(jnp.float32)
        b = theirs[j].astype(jnp.float32)
        first = jnp.where(is_first, a, b).reshape(8, 8, LANES)
        second = jnp.where(is_first, b, a).reshape(8, 8, LANES)
        block = jnp.stack([first, second], axis=1).reshape(LANES, LANES)
        if j < 12:
            col_out[j] = jnp.transpose(block).astype(bf16)
        else:
            lane = (j - 12) * LANES
            row_out[:, lane:lane + LANES] = block.astype(bf16)


def merge(mine, theirs):
    return local_call(merge_kernel, [(LANES, TILE), (12, LANES, LANES)], [mine, theirs])


def join_kernel(r0, r1, r2, r3, out):
    for o, ref in enumerate((r0, r1, r2, r3)):
        for s in range(4):
            for c in range(2):
                to = s * 128 + c * 64 + o * 16
                at = c * 64 + s * 16
                out[to:to + 16, :] = ref[at:at + 16, :]


def join(blocks):
    return local_call(join_kernel, [(512, TILE)], blocks)[0]


def back_kernel(tiles, own, other, c0, c1, c2a, c2b, c3, out, left, ready, sem):
    core = lax.axis_index("k")
    wide_at = pl.multiple_of(core * 64, 64)
    slim_at = pl.multiple_of((1 - core) * 128, 64)
    first = lax.broadcasted_iota(jnp.int32, (LANES, LANES), 1) < 64
    for s in range(4):
        for j in range(12):
            if s == 2:
                block = c2a[j] if j < 6 else c2b[j - 6]
            else:
                block = (c0, c1, None, c3)[s][j]
            moved = pltpu.roll(block.astype(jnp.float32), 64, 1)
            other_block = jnp.where(first, -moved, moved).astype(jnp.bfloat16)
            lanes = slice(s * LANES, (s + 1) * LANES)
            if j < 8:
                m = (j % 4) * 2 + j // 4
                left[m, pl.ds(wide_at, 128), lanes] = block
                left[m, pl.ds(QUARTER + wide_at, 128), lanes] = other_block
            else:
                for par in range(2):
                    m = (j - 8) * 2 + par
                    part = slice(par * 64, par * 64 + 64)
                    left[m, pl.ds(slim_at, 64), lanes] = block[part]
                    left[m, pl.ds(QUARTER + slim_at, 64), lanes] = other_block[part]

    def copy(slot):
        return pltpu.make_async_copy(ready.at[slot], out.at[0, 0, slot], sem.at[slot])

    def one(slot, carry):
        tile_row = tiles[0, 0, slot, 0]
        tile_col = tiles[0, 0, slot, 1]
        m = jnp.maximum(tile_col, 0) // 4
        u = (tile_row >= 16).astype(jnp.int32)

        def write(right):
            res = dot(left[m], right[...]) * 0.0625
            ready[slot, 0] = res[:QUARTER]
            ready[slot, 1] = res[QUARTER:]

        @pl.when(jnp.logical_and(tile_row >= 0, u == core))
        def _():
            write(own)

        @pl.when(jnp.logical_and(tile_row >= 0, u != core))
        def _():
            write(other)

        @pl.when(tile_row < 0)
        def _():
            ready[slot] = jnp.zeros((2, QUARTER, TILE), jnp.float32)

        copy(slot).start()
        return carry

    lax.fori_loop(0, SLOTS, one, 0)
    for slot in range(SLOTS):
        copy(slot).wait()


def back(tiles, *blocks):
    here = [pltpu.with_memory_space_constraint(b, pltpu.VMEM) for b in blocks]
    spec = pl.BlockSpec(memory_space=pltpu.VMEM)
    return pl.pallas_call(
        back_kernel,
        in_specs=[pl.BlockSpec(memory_space=pltpu.SMEM)] + [spec] * len(here),
        out_specs=pl.BlockSpec(memory_space=pl.ANY),
        scratch_shapes=[
            pltpu.VMEM((8, 2 * QUARTER, 512), jnp.bfloat16),
            pltpu.VMEM((SLOTS, 2, QUARTER, TILE), jnp.float32),
            pltpu.SemaphoreType.DMA((SLOTS,)),
        ],
        compiler_params=pltpu.CompilerParams(vmem_limit_bytes=28 << 20),
        out_shape=jax.ShapeDtypeStruct((1, 1, SLOTS, 2, QUARTER, TILE), jnp.float32),
        name="back",
    )(tiles, *here)


def swap(value, axis, bits):
    return lax.ppermute(value, axis, [(i, i ^ bits) for i in range(lax.axis_size(axis))])


def shift(value, by):
    return lax.ppermute(value, ("zh", "zl"), [(i, (i + by) % 8) for i in range(8)])


def body(fields, mirror_phase, tile_list):
    pieces = front(fields, mirror_phase)
    rows, cols = pieces[:4], pieces[4:]
    cols = [cols[0]] + [swap(cols[o], "x", o) for o in (1, 2, 3)]
    rows = [rows[0]] + [swap(rows[o], "y", o) for o in (1, 2, 3)]
    peers = pack(rows, cols)
    peers = [peers[0]] + [shift(peers[o], o) for o in range(1, 8)]
    mine, theirs = split(peers)
    theirs = swap(theirs, "k", 1)
    r0, c0 = merge(mine, theirs)
    c1 = swap(c0, "y", 1)
    c3 = swap(c0, "y", 3)
    r1 = swap(r0, "x", 1)
    r3 = swap(r0, "x", 3)
    c2a = swap(c3[:6], "y", 1)
    c2b = swap(c1[6:], "y", 3)
    r2 = swap(r3, "x", 1)
    own = join([r0, r1, r2, r3])
    other = swap(own, "k", 1)
    return back(tile_list, own, other, c0, c1, c2a, c2b, c3)


def solution(mesh):
    fine = Mesh(mesh.devices.reshape(2, 2, 4, 4, 4), AXES)
    in_specs = (P(AXES, None, None, None), P(), P(("zl", "y"), "x", None, None))
    out_specs = P(("zl", "y"), "x", None, None, ("zh", "k"), None)

    return jax.shard_map(body, mesh=fine, in_specs=in_specs, out_specs=out_specs, check_vma=False)
```

```python
import math

import jax
import jax.numpy as jnp
import numpy as np
from jax import lax
from jax.experimental import pallas as pl
from jax.experimental.pallas import tpu as pltpu
from jax.sharding import Mesh, PartitionSpec as P


NX = 512
NY = 256
TILE = 768
QUARTER = 192
SLOTS = 9
ROWS = 24
PEER_ROWS = 288
LANES = 128
AXES = ("zh", "k", "zl", "y", "x")


def dft_parts(length):
    positions = np.arange(length, dtype=np.int32)
    product = positions[:, None] * positions[None, :] % length
    angles = (np.float32(2.0 * math.pi / length) * product.astype(np.float32)).astype(np.float32)
    factor = np.float32(1.0 / math.sqrt(length))
    return np.cos(angles) * factor, np.sin(angles) * factor


def tables():
    bf16 = jnp.bfloat16
    cos_x, sin_x = dft_parts(NX)
    cos_y, sin_y = dft_parts(NY)
    inverse = np.zeros((192, 2 * NX), np.float32)
    turn = np.zeros((192, 192), np.float32)
    order = np.zeros((192, 192), np.float32)

    def place(tile, part, w):
        r, u = (tile, 0) if tile < 16 else (31 - tile, 1)
        return (((r % 4 * 4 + r // 4) * 2 + u) * 2 + part) * 3 + w

    for tile in range(32):
        for w in range(3):
            line = tile * 3 + w
            re, im = place(tile, 0, w), place(tile, 1, w)
            inverse[re] = np.concatenate([cos_x[line], -sin_x[line]])
            inverse[im] = np.concatenate([sin_x[line], cos_x[line]])
            turn[re, im] = -1.0
            turn[im, re] = 1.0
            for part in range(2):
                m, x = divmod(tile, 4)
                target = ((((w * 4 + x) * 2 + m % 2) * 4 + m // 2) * 2) + part
                order[target, place(tile, part, w)] = 1.0
    return [jnp.asarray(a, bf16) for a in (cos_x, sin_x, cos_y, sin_y, inverse, turn, order)]


def dot(a, b):
    return jnp.dot(a, b, preferred_element_type=jnp.float32)


def cos_sin(theta):
    h = theta * 0.5
    s = h * h
    sin_h = h * (1.0 + s * (-1.0 / 6 + s * (1.0 / 120 + s * (-1.0 / 5040 + s * (1.0 / 362880 + s * (-1.0 / 39916800))))))
    cos_h = 1.0 + s * (-0.5 + s * (1.0 / 24 + s * (-1.0 / 720 + s * (1.0 / 40320 + s * (-1.0 / 3628800 + s * (1.0 / 479001600))))))
    return 1.0 - 2.0 * sin_h * sin_h, 2.0 * sin_h * cos_h


def front_kernel(fields, phase, cos_x, sin_x, cos_y, sin_y, inverse, turn, order, keep, give, slab_f, slab_c):
    bf16 = jnp.bfloat16
    xr = fields[0, 0]
    xi = fields[0, 1]
    cx = cos_x[...]
    sx = sin_x[...]
    first_r = (dot(cx, xr) + dot(sx, xi)).astype(bf16)
    first_i = (dot(cx, xi) - dot(sx, xr)).astype(bf16)
    cy = cos_y[...]
    sy = sin_y[...]
    turned_r = dot(first_r, cy) + dot(first_i, sy)
    turned_i = dot(first_i, cy) - dot(first_r, sy)
    cos_p, sin_p = cos_sin(phase[...])
    spec_r = (turned_r * cos_p - turned_i * sin_p).astype(bf16)
    spec_i = (turned_r * sin_p + turned_i * cos_p).astype(bf16)
    inv = inverse[...]
    back = (dot(inv[:, :NX], spec_r) + dot(inv[:, NX:], spec_i)).astype(bf16)
    back_turned = dot(turn[...], back).astype(bf16)
    slab = (dot(back, cy) + dot(back_turned, sy)).astype(bf16)
    slab_f[...] = slab.astype(jnp.float32)
    slab_c[...] = dot(order[...], slab)
    x_at = lax.axis_index("x")
    y_at = lax.axis_index("y")
    low = lax.broadcasted_iota(jnp.int32, (8, LANES), 1) < 64
    wide = ((0, 0), (1, 0), (1, 1), (2, 1))
    slim = ((0, 1), (0, 1), (2, 0), (2, 0))
    core = lax.axis_index("k")

    def put_rows(out):
        for o in range(4):
            block = slab_f[pl.ds(pl.multiple_of((y_at ^ o) * 48, 8), 48), :]
            for zl in range(4):
                for u in range(2):
                    for h in range(2):
                        at = (zl * 2 + u) * 6
                        to = u * 12 + h * 6
                        out[o * 4 + zl, to:to + 6, :] = block[at:at + 6, h * LANES:(h + 1) * LANES].astype(bf16)

    def put_cols(out):
        for o in range(4):
            xb = (x_at ^ o) * 16
            for q in range(4):
                w, h = wide[q]
                a = slab_c[pl.ds(pl.multiple_of(xb + w * 64, 8), 16), h * LANES:(h + 1) * LANES]
                w, h = slim[q]
                e = slab_c[pl.ds(pl.multiple_of(xb + w * 64, 8), 16), h * LANES:(h + 1) * LANES]
                even, odd = e[:8], e[8:]
                if q % 2 == 0:
                    b = jnp.where(low, even, pltpu.roll(odd, 64, 1))
                else:
                    b = jnp.where(low, pltpu.roll(even, 64, 1), odd)
                out[o * 4 + q, 0:16, :] = a.astype(bf16)
                out[o * 4 + q, 16:24, :] = b.astype(bf16)

    @pl.when(core == 0)
    def _():
        put_rows(keep)
        put_cols(give)

    @pl.when(core == 1)
    def _():
        put_cols(keep)
        put_rows(give)


def vmem(shape, dtype=jnp.bfloat16):
    return pltpu.VMEM(shape, dtype)


def local_call(kernel, outs, args, scratch=()):
    spec = pl.BlockSpec(memory_space=pltpu.VMEM)
    here = [pltpu.with_memory_space_constraint(a, pltpu.VMEM) for a in args]
    return pl.pallas_call(
        kernel,
        out_shape=[vmem(shape) for shape in outs],
        in_specs=[spec] * len(here),
        out_specs=[spec] * len(outs),
        scratch_shapes=list(scratch),
        compiler_params=pltpu.CompilerParams(vmem_limit_bytes=12 << 20),
    )(*here)


def front(fields, phase):
    return pl.pallas_call(
        front_kernel,
        out_shape=[vmem((16, ROWS, LANES))] * 2,
        out_specs=[pl.BlockSpec(memory_space=pltpu.VMEM)] * 2,
        scratch_shapes=[pltpu.VMEM((192, NY), jnp.float32), pltpu.VMEM((192, NY), jnp.float32)],
        name="front",
    )(fields, phase, *tables())


def lay_kernel(keep, got, *outs):
    is_first = lax.axis_index("k") == 0

    @pl.when(is_first)
    def _():
        for o, out in enumerate(outs):
            out[0:4] = keep[o * 4:o * 4 + 4]
            out[4:8] = got[o * 4:o * 4 + 4]

    @pl.when(jnp.logical_not(is_first))
    def _():
        for o, out in enumerate(outs):
            out[0:4] = got[o * 4:o * 4 + 4]
            out[4:8] = keep[o * 4:o * 4 + 4]


def lay(keep, got):
    return local_call(lay_kernel, [(8, ROWS, LANES)] * 4, [keep, got])


def stack_kernel(*refs):
    out = refs[4]
    for o in range(4):
        out[o * 8:o * 8 + 8] = refs[o][...]


def stack(parts):
    return local_call(stack_kernel, [(32, ROWS, LANES)], parts)[0]


def pack_kernel(mine, other, z1, z2, z3, z4, home):
    core = lax.axis_index("k")
    z_at = lax.axis_index("zh") * 4 + lax.axis_index("zl")

    def fill(out, z, rows, cols, electrons):
        zh = z // 4
        zl = z % 4
        for i, e in enumerate(electrons):
            for o in range(4):
                at = (o * 2 + e) * 4
                for k in range(2):
                    to = i * PEER_ROWS + o * 48 + k * 24
                    out[to:to + 24, :] = cols[at + zh * 2 + k]
                to = i * PEER_ROWS + 192 + o * 24
                out[to:to + 24, :] = rows[at + zl]

    def fill_all(rows, cols, sign, e):
        for d, out in ((1, z1), (2, z2), (3, z3)):
            fill(out, (z_at + sign * d + 8) % 8, rows, cols, (0, 1))
        fill(z4, (z_at + 4) % 8, rows, cols, (e,))
        fill(home, z_at, rows, cols, (e,))

    @pl.when(core == 0)
    def _():
        fill_all(mine, other, 1, 0)

    @pl.when(core == 1)
    def _():
        fill_all(other, mine, -1, 1)


def pack(mine, other):
    return local_call(pack_kernel, [(2 * PEER_ROWS, LANES)] * 3 + [(PEER_ROWS, LANES)] * 2, [mine, other])


def split_kernel(*refs):
    peers = refs[:5]
    mine, theirs, flat = refs[5:]
    bf16 = jnp.bfloat16
    core = lax.axis_index("k")
    at = 0
    for peer in peers:
        flat[at:at + peer.shape[0], :] = peer[...].astype(jnp.float32)
        at += peer.shape[0]

    def pair(at, step):
        return jnp.concatenate(
            [flat[pl.ds(at, 8, stride=PEER_ROWS), :], flat[pl.ds(at + step, 8, stride=PEER_ROWS), :]], axis=0
        ).astype(bf16)

    for out, k in ((mine, core), (theirs, 1 - core)):
        for c in range(2):
            for o in range(0, 4, 2):
                to = (c * 4 + o) * 8
                for j in range(12):
                    out[j, to:to + 16, :] = pair(o * 48 + k * 24 + j * 2 + c, 48)
                for w in range(3):
                    for h in range(2):
                        out[12 + w * 2 + h, to:to + 16, :] = pair(192 + o * 24 + k * 12 + h * 6 + c * 3 + w, 24)


def split(peers):
    return local_call(
        split_kernel, [(18, 64, LANES)] * 2, peers, scratch=[pltpu.VMEM((8 * PEER_ROWS, LANES), jnp.float32)]
    )


def merge_kernel(mine, theirs, row_out, col_out):
    bf16 = jnp.bfloat16
    is_first = lax.axis_index("k") == 0
    for j in range(18):
        a = mine[j].astype(jnp.float32)
        b = theirs[j].astype(jnp.float32)
        first = jnp.where(is_first, a, b).reshape(8, 8, LANES)
        second = jnp.where(is_first, b, a).reshape(8, 8, LANES)
        block = jnp.stack([first, second], axis=1).reshape(LANES, LANES)
        if j < 12:
            col_out[j] = jnp.transpose(block).astype(bf16)
        else:
            lane = (j - 12) * LANES
            row_out[:, lane:lane + LANES] = block.astype(bf16)


def merge(mine, theirs):
    return local_call(merge_kernel, [(LANES, TILE), (12, LANES, LANES)], [mine, theirs])


def join_kernel(r0, r1, r2, r3, out):
    for o, ref in enumerate((r0, r1, r2, r3)):
        for s in range(4):
            for c in range(2):
                to = s * 128 + c * 64 + o * 16
                at = c * 64 + s * 16
                out[to:to + 16, :] = ref[at:at + 16, :]


def join(blocks):
    return local_call(join_kernel, [(512, TILE)], blocks)[0]


def back_kernel(tiles, own, other, c0, c1, c2a, c2b, c3, out, left, ready, sem):
    core = lax.axis_index("k")
    wide_at = pl.multiple_of(core * 64, 64)
    slim_at = pl.multiple_of((1 - core) * 128, 64)
    first = lax.broadcasted_iota(jnp.int32, (LANES, LANES), 1) < 64
    for s in range(4):
        for j in range(12):
            if s == 2:
                block = c2a[j] if j < 6 else c2b[j - 6]
            else:
                block = (c0, c1, None, c3)[s][j]
            moved = pltpu.roll(block.astype(jnp.float32), 64, 1)
            other_block = jnp.where(first, -moved, moved).astype(jnp.bfloat16)
            lanes = slice(s * LANES, (s + 1) * LANES)
            if j < 8:
                m = (j % 4) * 2 + j // 4
                left[m, pl.ds(wide_at, 128), lanes] = block
                left[m, pl.ds(QUARTER + wide_at, 128), lanes] = other_block
            else:
                for par in range(2):
                    m = (j - 8) * 2 + par
                    part = slice(par * 64, par * 64 + 64)
                    left[m, pl.ds(slim_at, 64), lanes] = block[part]
                    left[m, pl.ds(QUARTER + slim_at, 64), lanes] = other_block[part]

    def copy(slot):
        return pltpu.make_async_copy(ready.at[slot], out.at[0, 0, slot], sem.at[slot])

    def one(slot, carry):
        tile_row = tiles[0, 0, slot, 0]
        tile_col = tiles[0, 0, slot, 1]
        m = jnp.maximum(tile_col, 0) // 4
        u = (tile_row >= 16).astype(jnp.int32)

        def write(right):
            res = dot(left[m], right[...]) * 0.0625
            ready[slot, 0] = res[:QUARTER]
            ready[slot, 1] = res[QUARTER:]

        @pl.when(jnp.logical_and(tile_row >= 0, u == core))
        def _():
            write(own)

        @pl.when(jnp.logical_and(tile_row >= 0, u != core))
        def _():
            write(other)

        @pl.when(tile_row < 0)
        def _():
            ready[slot] = jnp.zeros((2, QUARTER, TILE), jnp.float32)

        copy(slot).start()
        return carry

    lax.fori_loop(0, SLOTS, one, 0)
    for slot in range(SLOTS):
        copy(slot).wait()


def back(tiles, *blocks):
    here = [pltpu.with_memory_space_constraint(b, pltpu.VMEM) for b in blocks]
    spec = pl.BlockSpec(memory_space=pltpu.VMEM)
    return pl.pallas_call(
        back_kernel,
        in_specs=[pl.BlockSpec(memory_space=pltpu.SMEM)] + [spec] * len(here),
        out_specs=pl.BlockSpec(memory_space=pl.ANY),
        scratch_shapes=[
            pltpu.VMEM((8, 2 * QUARTER, 512), jnp.bfloat16),
            pltpu.VMEM((SLOTS, 2, QUARTER, TILE), jnp.float32),
            pltpu.SemaphoreType.DMA((SLOTS,)),
        ],
        compiler_params=pltpu.CompilerParams(vmem_limit_bytes=28 << 20),
        out_shape=jax.ShapeDtypeStruct((1, 1, SLOTS, 2, QUARTER, TILE), jnp.float32),
        name="back",
    )(tiles, *here)


def swap(value, axis, bits):
    return lax.ppermute(value, axis, [(i, i ^ bits) for i in range(lax.axis_size(axis))])


def coordinates(device):
    return dict(x=device % 4, y=device // 4 % 4, z=device // 16 % 4 + device // 128 * 4, k=device // 64 % 2)


def move(value, change):
    pairs = []
    for device in range(256):
        at = coordinates(device)
        to = {**at, **change(**at)}
        pairs.append((device, (((to["z"] // 4 * 2 + to["k"]) * 4 + to["z"] % 4) * 4 + to["y"]) * 4 + to["x"]))
    return lax.ppermute(value, AXES, pairs)


def body(fields, mirror_phase, tile_list):
    keep, give = front(fields, mirror_phase)
    got = swap(give, "k", 1)
    parts = lay(keep, got)

    def scatter(o):
        return lambda x, y, k, **at: {"y": y ^ o} if k == 0 else {"x": x ^ o}

    parts = [parts[0]] + [move(parts[o], scatter(o)) for o in (1, 2, 3)]
    mine = stack(parts)
    other = swap(mine, "k", 1)

    def along(d):
        return lambda z, k, **at: {"z": (z + (d if k == 0 else -d)) % 8}

    z1, z2, z3, z4, home = pack(mine, other)
    z1, z2, z3, z4 = [move(v, along(d)) for d, v in ((1, z1), (2, z2), (3, z3), (4, z4))]
    mine, theirs = split([z1, z2, z3, home, z4])
    theirs = swap(theirs, "k", 1)
    r0, c0 = merge(mine, theirs)
    c1 = swap(c0, "y", 1)
    c3 = swap(c0, "y", 3)
    r1 = swap(r0, "x", 1)
    r3 = swap(r0, "x", 3)
    c2a = swap(c3[:6], "y", 1)
    c2b = swap(c1[6:], "y", 3)
    r2 = swap(r3, "x", 1)
    own = join([r0, r1, r2, r3])
    other = swap(own, "k", 1)
    return back(tile_list, own, other, c0, c1, c2a, c2b, c3)


def solution(mesh):
    fine = Mesh(mesh.devices.reshape(2, 2, 4, 4, 4), AXES)
    in_specs = (P(AXES, None, None, None), P(), P(("zl", "y"), "x", None, None))
    out_specs = P(("zl", "y"), "x", None, None, ("zh", "k"), None)

    return jax.shard_map(body, mesh=fine, in_specs=in_specs, out_specs=out_specs, check_vma=False)
```

```python
import math

import jax
import jax.numpy as jnp
import numpy as np
from jax import lax
from jax.experimental import pallas as pl
from jax.experimental.pallas import tpu as pltpu
from jax.sharding import Mesh, PartitionSpec as P


NX = 512
NY = 256
TILE = 768
QUARTER = 192
SLOTS = 9
ROWS = 24
PEER_ROWS = 288
LANES = 128
AXES = ("zh", "k", "zl", "y", "x")


def dft_parts(length):
    positions = np.arange(length, dtype=np.int32)
    product = positions[:, None] * positions[None, :] % length
    angles = (np.float32(2.0 * math.pi / length) * product.astype(np.float32)).astype(np.float32)
    factor = np.float32(1.0 / math.sqrt(length))
    return np.cos(angles) * factor, np.sin(angles) * factor


def tables():
    bf16 = jnp.bfloat16
    cos_x, sin_x = dft_parts(NX)
    cos_y, sin_y = dft_parts(NY)
    inverse = np.zeros((192, 2 * NX), np.float32)
    turn = np.zeros((192, 192), np.float32)
    order = np.zeros((192, 192), np.float32)

    def place(tile, part, w):
        r, u = (tile, 0) if tile < 16 else (31 - tile, 1)
        return (((r % 4 * 4 + r // 4) * 2 + u) * 2 + part) * 3 + w

    for tile in range(32):
        for w in range(3):
            line = tile * 3 + w
            re, im = place(tile, 0, w), place(tile, 1, w)
            inverse[re] = np.concatenate([cos_x[line], -sin_x[line]])
            inverse[im] = np.concatenate([sin_x[line], cos_x[line]])
            turn[re, im] = -1.0
            turn[im, re] = 1.0
            for part in range(2):
                m, x = divmod(tile, 4)
                target = ((((w * 4 + x) * 2 + m % 2) * 4 + m // 2) * 2) + part
                order[target, place(tile, part, w)] = 1.0
    return [jnp.asarray(a, bf16) for a in (cos_x, sin_x, cos_y, sin_y, inverse, turn, order)]


def dot(a, b):
    return jnp.dot(a, b, preferred_element_type=jnp.float32)


def cos_sin(theta):
    h = theta * 0.5
    s = h * h
    sin_h = h * (1.0 + s * (-1.0 / 6 + s * (1.0 / 120 + s * (-1.0 / 5040 + s * (1.0 / 362880 + s * (-1.0 / 39916800))))))
    cos_h = 1.0 + s * (-0.5 + s * (1.0 / 24 + s * (-1.0 / 720 + s * (1.0 / 40320 + s * (-1.0 / 3628800 + s * (1.0 / 479001600))))))
    return 1.0 - 2.0 * sin_h * sin_h, 2.0 * sin_h * cos_h


def front_kernel(fields, phase, cos_x, sin_x, cos_y, sin_y, inverse, turn, order, keep, give, slab_f, slab_c):
    bf16 = jnp.bfloat16
    xr = fields[0, 0]
    xi = fields[0, 1]
    cx = cos_x[...]
    sx = sin_x[...]
    first_r = (dot(cx, xr) + dot(sx, xi)).astype(bf16)
    first_i = (dot(cx, xi) - dot(sx, xr)).astype(bf16)
    cy = cos_y[...]
    sy = sin_y[...]
    turned_r = dot(first_r, cy) + dot(first_i, sy)
    turned_i = dot(first_i, cy) - dot(first_r, sy)
    cos_p, sin_p = cos_sin(phase[...])
    spec_r = (turned_r * cos_p - turned_i * sin_p).astype(bf16)
    spec_i = (turned_r * sin_p + turned_i * cos_p).astype(bf16)
    inv = inverse[...]
    back = (dot(inv[:, :NX], spec_r) + dot(inv[:, NX:], spec_i)).astype(bf16)
    back_turned = dot(turn[...], back).astype(bf16)
    slab = (dot(back, cy) + dot(back_turned, sy)).astype(bf16)
    slab_f[...] = slab.astype(jnp.float32)
    slab_c[...] = dot(order[...], slab)
    x_at = lax.axis_index("x")
    y_at = lax.axis_index("y")
    low = lax.broadcasted_iota(jnp.int32, (8, LANES), 1) < 64
    wide = ((0, 0), (1, 0), (1, 1), (2, 1))
    slim = ((0, 1), (0, 1), (2, 0), (2, 0))
    core = lax.axis_index("k")

    def put_rows(out):
        for o in range(4):
            block = slab_f[pl.ds(pl.multiple_of((y_at ^ o) * 48, 8), 48), :]
            for zl in range(4):
                for u in range(2):
                    for h in range(2):
                        at = (zl * 2 + u) * 6
                        to = u * 12 + h * 6
                        out[o * 4 + zl, to:to + 6, :] = block[at:at + 6, h * LANES:(h + 1) * LANES].astype(bf16)

    def put_cols(out):
        for o in range(4):
            xb = (x_at ^ o) * 16
            for q in range(4):
                w, h = wide[q]
                a = slab_c[pl.ds(pl.multiple_of(xb + w * 64, 8), 16), h * LANES:(h + 1) * LANES]
                w, h = slim[q]
                e = slab_c[pl.ds(pl.multiple_of(xb + w * 64, 8), 16), h * LANES:(h + 1) * LANES]
                even, odd = e[:8], e[8:]
                if q % 2 == 0:
                    b = jnp.where(low, even, pltpu.roll(odd, 64, 1))
                else:
                    b = jnp.where(low, pltpu.roll(even, 64, 1), odd)
                out[o * 4 + q, 0:16, :] = a.astype(bf16)
                out[o * 4 + q, 16:24, :] = b.astype(bf16)

    @pl.when(core == 0)
    def _():
        put_rows(keep)
        put_cols(give)

    @pl.when(core == 1)
    def _():
        put_cols(keep)
        put_rows(give)


def vmem(shape, dtype=jnp.bfloat16):
    return pltpu.VMEM(shape, dtype)


def local_call(kernel, outs, args, scratch=()):
    spec = pl.BlockSpec(memory_space=pltpu.VMEM)
    here = [pltpu.with_memory_space_constraint(a, pltpu.VMEM) for a in args]
    return pl.pallas_call(
        kernel,
        out_shape=[vmem(shape) for shape in outs],
        in_specs=[spec] * len(here),
        out_specs=[spec] * len(outs),
        scratch_shapes=list(scratch),
        compiler_params=pltpu.CompilerParams(vmem_limit_bytes=12 << 20),
    )(*here)


def front(fields, phase):
    return pl.pallas_call(
        front_kernel,
        out_shape=[vmem((16, ROWS, LANES))] * 2,
        out_specs=[pl.BlockSpec(memory_space=pltpu.VMEM)] * 2,
        scratch_shapes=[pltpu.VMEM((192, NY), jnp.float32), pltpu.VMEM((192, NY), jnp.float32)],
        name="front",
    )(fields, phase, *tables())


def lay_kernel(keep, got, *outs):
    is_first = lax.axis_index("k") == 0

    @pl.when(is_first)
    def _():
        for o, out in enumerate(outs):
            out[0:4] = keep[o * 4:o * 4 + 4]
            out[4:8] = got[o * 4:o * 4 + 4]

    @pl.when(jnp.logical_not(is_first))
    def _():
        for o, out in enumerate(outs):
            out[0:4] = got[o * 4:o * 4 + 4]
            out[4:8] = keep[o * 4:o * 4 + 4]


def lay(keep, got):
    return local_call(lay_kernel, [(8, ROWS, LANES)] * 4, [keep, got])


def stack_kernel(*refs):
    out = refs[4]
    for o in range(4):
        out[o * 8:o * 8 + 8] = refs[o][...]


def stack(parts):
    return local_call(stack_kernel, [(32, ROWS, LANES)], parts)[0]


def pack_kernel(mine, other, z1, z2, z3, z4, home):
    core = lax.axis_index("k")
    z_at = lax.axis_index("zh") * 4 + lax.axis_index("zl")

    def fill(out, z, rows, cols, electrons):
        zh = z // 4
        zl = z % 4
        for i, e in enumerate(electrons):
            for o in range(4):
                at = (o * 2 + e) * 4
                for k in range(2):
                    to = i * PEER_ROWS + o * 48 + k * 24
                    out[to:to + 24, :] = cols[at + zh * 2 + k]
                to = i * PEER_ROWS + 192 + o * 24
                out[to:to + 24, :] = rows[at + zl]

    def fill_all(rows, cols, sign, e):
        for d, out in ((1, z1), (2, z2), (3, z3)):
            fill(out, (z_at + sign * d + 8) % 8, rows, cols, (0, 1))
        fill(z4, (z_at + 4) % 8, rows, cols, (e,))
        fill(home, z_at, rows, cols, (e,))

    @pl.when(core == 0)
    def _():
        fill_all(mine, other, 1, 0)

    @pl.when(core == 1)
    def _():
        fill_all(other, mine, -1, 1)


def pack(mine, other):
    return local_call(pack_kernel, [(2 * PEER_ROWS, LANES)] * 3 + [(PEER_ROWS, LANES)] * 2, [mine, other])


def split_kernel(*refs):
    peers = refs[:5]
    mine, theirs, flat = refs[5:]
    bf16 = jnp.bfloat16
    core = lax.axis_index("k")
    at = 0
    for peer in peers:
        flat[at:at + peer.shape[0], :] = peer[...].astype(jnp.float32)
        at += peer.shape[0]

    def pair(at, step):
        return jnp.concatenate(
            [flat[pl.ds(at, 8, stride=PEER_ROWS), :], flat[pl.ds(at + step, 8, stride=PEER_ROWS), :]], axis=0
        ).astype(bf16)

    for out, k in ((mine, core), (theirs, 1 - core)):
        for c in range(2):
            for o in range(0, 4, 2):
                to = (c * 4 + o) * 8
                for j in range(12):
                    out[j, to:to + 16, :] = pair(o * 48 + k * 24 + j * 2 + c, 48)
                for w in range(3):
                    for h in range(2):
                        out[12 + w * 2 + h, to:to + 16, :] = pair(192 + o * 24 + k * 12 + h * 6 + c * 3 + w, 24)


def split(peers):
    return local_call(
        split_kernel, [(18, 64, LANES)] * 2, peers, scratch=[pltpu.VMEM((8 * PEER_ROWS, LANES), jnp.float32)]
    )


def merge_kernel(mine, theirs, row_out, col_out):
    bf16 = jnp.bfloat16
    is_first = lax.axis_index("k") == 0
    for j in range(18):
        a = mine[j].astype(jnp.float32)
        b = theirs[j].astype(jnp.float32)
        first = jnp.where(is_first, a, b).reshape(8, 8, LANES)
        second = jnp.where(is_first, b, a).reshape(8, 8, LANES)
        block = jnp.stack([first, second], axis=1).reshape(LANES, LANES)
        if j < 12:
            col_out[j] = jnp.transpose(block).astype(bf16)
        else:
            lane = (j - 12) * LANES
            row_out[:, lane:lane + LANES] = block.astype(bf16)


def merge(mine, theirs):
    return local_call(merge_kernel, [(LANES, TILE), (12, LANES, LANES)], [mine, theirs])


def join_kernel(r0, r1, r2, r3, out):
    for o, ref in enumerate((r0, r1, r2, r3)):
        for s in range(4):
            for c in range(2):
                to = s * 128 + c * 64 + o * 16
                at = c * 64 + s * 16
                out[to:to + 16, :] = ref[at:at + 16, :]


def join(blocks):
    return local_call(join_kernel, [(512, TILE)], blocks)[0]


def back_kernel(tiles, own, other, c0, c1, c2a, c2b, c3, out, left, ready, right, sem):
    right[0] = own[...]
    right[1] = other[...]
    core = lax.axis_index("k")
    wide_at = pl.multiple_of(core * 64, 64)
    slim_at = pl.multiple_of((1 - core) * 128, 64)
    first = lax.broadcasted_iota(jnp.int32, (LANES, LANES), 1) < 64
    for s in range(4):
        for j in range(12):
            if s == 2:
                block = c2a[j] if j < 6 else c2b[j - 6]
            else:
                block = (c0, c1, None, c3)[s][j]
            moved = pltpu.roll(block.astype(jnp.float32), 64, 1)
            other_block = jnp.where(first, -moved, moved).astype(jnp.bfloat16)
            lanes = slice(s * LANES, (s + 1) * LANES)
            if j < 8:
                m = (j % 4) * 2 + j // 4
                left[m, pl.ds(wide_at, 128), lanes] = block
                left[m, pl.ds(QUARTER + wide_at, 128), lanes] = other_block
            else:
                for par in range(2):
                    m = (j - 8) * 2 + par
                    part = slice(par * 64, par * 64 + 64)
                    left[m, pl.ds(slim_at, 64), lanes] = block[part]
                    left[m, pl.ds(QUARTER + slim_at, 64), lanes] = other_block[part]

    def copy(slot):
        return pltpu.make_async_copy(ready.at[slot], out.at[0, 0, slot], sem.at[slot])

    def one(slot, carry):
        tile_row = tiles[0, 0, slot, 0]
        tile_col = tiles[0, 0, slot, 1]
        m = jnp.maximum(tile_col, 0) // 4
        u = (tile_row >= 16).astype(jnp.int32)

        scale = jnp.where(tile_row >= 0, 0.0625, 0.0)
        res = dot(left[m], right[jnp.where(u == core, 0, 1)]) * scale
        ready[slot, 0] = res[:QUARTER]
        ready[slot, 1] = res[QUARTER:]
        copy(slot).start()
        return carry

    lax.fori_loop(0, SLOTS, one, 0, unroll=3)
    for slot in range(SLOTS):
        copy(slot).wait()


def back(tiles, *blocks):
    here = [pltpu.with_memory_space_constraint(b, pltpu.VMEM) for b in blocks]
    spec = pl.BlockSpec(memory_space=pltpu.VMEM)
    return pl.pallas_call(
        back_kernel,
        in_specs=[pl.BlockSpec(memory_space=pltpu.SMEM)] + [spec] * len(here),
        out_specs=pl.BlockSpec(memory_space=pl.ANY),
        scratch_shapes=[
            pltpu.VMEM((8, 2 * QUARTER, 512), jnp.bfloat16),
            pltpu.VMEM((SLOTS, 2, QUARTER, TILE), jnp.float32),
            pltpu.VMEM((2, 512, TILE), jnp.bfloat16),
            pltpu.SemaphoreType.DMA((SLOTS,)),
        ],
        compiler_params=pltpu.CompilerParams(vmem_limit_bytes=28 << 20),
        out_shape=jax.ShapeDtypeStruct((1, 1, SLOTS, 2, QUARTER, TILE), jnp.float32),
        name="back",
    )(tiles, *here)


def swap(value, axis, bits):
    return lax.ppermute(value, axis, [(i, i ^ bits) for i in range(lax.axis_size(axis))])


def coordinates(device):
    return dict(x=device % 4, y=device // 4 % 4, z=device // 16 % 4 + device // 128 * 4, k=device // 64 % 2)


def move(value, change):
    pairs = []
    for device in range(256):
        at = coordinates(device)
        to = {**at, **change(**at)}
        pairs.append((device, (((to["z"] // 4 * 2 + to["k"]) * 4 + to["z"] % 4) * 4 + to["y"]) * 4 + to["x"]))
    return lax.ppermute(value, AXES, pairs)


def body(fields, mirror_phase, tile_list):
    keep, give = front(fields, mirror_phase)
    got = swap(give, "k", 1)
    parts = lay(keep, got)

    def scatter(o):
        return lambda x, y, k, **at: {"y": y ^ o} if k == 0 else {"x": x ^ o}

    parts = [parts[0]] + [move(parts[o], scatter(o)) for o in (1, 2, 3)]
    mine = stack(parts)
    other = swap(mine, "k", 1)

    def along(d):
        return lambda z, k, **at: {"z": (z + (d if k == 0 else -d)) % 8}

    z1, z2, z3, z4, home = pack(mine, other)
    z1, z2, z3, z4 = [move(v, along(d)) for d, v in ((1, z1), (2, z2), (3, z3), (4, z4))]
    mine, theirs = split([z1, z2, z3, home, z4])
    theirs = swap(theirs, "k", 1)
    r0, c0 = merge(mine, theirs)
    c1 = swap(c0, "y", 1)
    c3 = swap(c0, "y", 3)
    r1 = swap(r0, "x", 1)
    r3 = swap(r0, "x", 3)
    c2a = swap(c3[:6], "y", 1)
    c2b = swap(c1[6:], "y", 3)
    r2 = swap(r3, "x", 1)
    own = join([r0, r1, r2, r3])
    other = swap(own, "k", 1)
    return back(tile_list, own, other, c0, c1, c2a, c2b, c3)


def solution(mesh):
    fine = Mesh(mesh.devices.reshape(2, 2, 4, 4, 4), AXES)
    in_specs = (P(AXES, None, None, None), P(), P(("zl", "y"), "x", None, None))
    out_specs = P(("zl", "y"), "x", None, None, ("zh", "k"), None)

    return jax.shard_map(body, mesh=fine, in_specs=in_specs, out_specs=out_specs, check_vma=False)
```
